32 devices in a mesh: mem: 8 (over y, x, core), reg: 4 (over z).
Axes of the slice: x: 2, y: 2, z: 4, core: 2. Of those that a mesh axis runs over, the one named last changes fastest.
Arguments:
- ens_state: bfloat16 [128, 16384], P('mem', 'reg'), may hold values from -6 to 6
- ens_obs: bfloat16 [128, 8192], P('mem', 'reg'), may hold values from -6 to 6
- innov: bfloat16 [128, 8192], P('mem', 'reg'), may hold values from -6 to 6
- state_coord: int32 [2, 16384], P(None, 'reg'), may hold values from 0 to 63
- obs_coord: int32 [2, 8192], replicated, may hold values from 0 to 63
- obs_routes: int32 [64, 1], replicated, may hold values from 0 to 3; in each aligned block of 16 rows (0 to 15, 16 to 31, ...) at most 8 rows name the same one
Outputs:
- analysis: bfloat16 [128, 16384], P('mem', 'reg')
The draws below stay inside these ranges and needn't reach their ends.
Inputs may be any that keep to these rules, and one draw needn't show every extreme that they name: `obs_routes`: in each aligned block of 16 rows (the observation blocks of one source region) no region is named by more than 8 rows, a bound that some block reaches.
All inputs are finite; a program needn't handle non-finite values.
Results may differ from the reference program's by a relative error of at most 0.0022.
The reference program's roundings to bfloat16 on the way (of `state_anom`, `obs_anom`, `tiles` and `increments`) count: a program that leaves them out, or rounds other values in their place, can miss the bound.
Values may be sent and summed in bfloat16 or wider, within the bound.
No kernel may reach another device: no remote copies, remote signals or barrier semaphores. Data moves between devices by JAX's collectives and lax.ppermute only.
A program may use at most 64 MiB of HBM per device.

```python
import math
import jax
import jax.numpy as jnp
import numpy as np
from jax import lax

BLK = 128
SB_DEV = 4
LOC = 32
REGIONS = 4
BANDS = 8
MEMBERS = 128
STATE_REG = 4096
STATE = 16384
SLOTS = 4
OBK_REG = 16
NOBK = 64
NOBS = 8192
CAP = 8
N_REG = 4


def ensemble_draw(key, columns):
    key_mean = jax.random.fold_in(key, 0)
    key_spread = jax.random.fold_in(key, 2)
    center = jax.random.uniform(key_mean, (1, columns), jnp.float32, -1.5, 1.5)
    spread = jnp.clip(jax.random.normal(key_spread, (MEMBERS, columns), jnp.float32), -4.0, 4.0)
    return jnp.clip(center + spread, -6.0, 6.0).astype(jnp.bfloat16)


def draw_ens_state(key, part):
    return ensemble_draw(jax.random.fold_in(key, 11), STATE)


def draw_ens_obs(key, part):
    return ensemble_draw(jax.random.fold_in(key, 23), NOBS)


def place_ends(entries, own_key, smallest, high):
    longest = entries.shape.index(max(entries.shape))
    spots = []
    for shift in (0, 1):
        where = [jax.random.randint(jax.random.fold_in(own_key, axis), (), 0, length) for axis, length in enumerate(entries.shape)]
        where[longest] = (where[longest] + shift) % entries.shape[longest]
        spots.append(tuple(where))
    return entries.at[spots[0]].set(smallest).at[spots[1]].set(high)


def shard_levels(rng, dims, cuts, least, largest):
    factor_of, own = 1.0, jax.random.fold_in(rng, 6)
    for axis_at, shards_of in cuts:
        heights = jnp.exp(jax.random.uniform(jax.random.fold_in(own, axis_at), (shards_of,), jnp.float32, least / len(cuts), largest / len(cuts)))
        factor_of = factor_of * jnp.repeat(heights, dims[axis_at] // shards_of).reshape([-1 if axis == axis_at else 1 for axis in range(len(dims))])
    return factor_of


def assign_block(rng, own, number, rows, number_of, top, bound, lean):
    sequence = jax.random.permutation(rng, number_of)
    crowded, common = load_shares(number_of, rows * top, bound, lean, True), load_shares(number_of, rows * top, bound, lean, False)
    places = jnp.arange(number_of)

    def named(lengths, offset_by):
        used = int((lengths > 0).sum())
        fixed = max(1, used // 4)
        moved = fixed + (places - fixed + offset_by * (used - fixed)) % max(1, number_of - fixed)
        return jnp.zeros((number_of,), jnp.int32).at[sequence[jnp.where(places < fixed, places, moved)]].set(jnp.asarray(lengths, jnp.int32))

    lengths = jnp.where(number % 4 == 0, named(crowded, number // 4), named(common, number - number // 4 - 1))
    mixed = jax.random.permutation(jax.random.fold_in(own, 3), number_of)
    giver, sink = mixed[0:number_of // 2 * 2:2], mixed[1:number_of // 2 * 2:2]
    room = jnp.minimum(lengths[giver] - 1, bound - lengths[sink]) // 2
    room = jnp.where((giver == sequence[0]) | (sink == sequence[0]) | (lengths[sink] == 0), 0, jnp.maximum(room, 0))
    moved = jax.random.randint(jax.random.fold_in(own, 4), (number_of // 2,), 0, 1 << 20) % (room + 1)
    lengths = lengths.at[giver].add(-moved).at[sink].add(moved)
    labels = jnp.searchsorted(jnp.cumsum(lengths), jnp.arange(rows * top), side="right").astype(jnp.int32)
    listing = labels.reshape(top, rows).T
    listing = listing[jax.random.permutation(jax.random.fold_in(own, 1), rows)]
    offset_by = jax.random.randint(jax.random.fold_in(own, 2), (rows, 1), 0, top)
    return jnp.take_along_axis(listing, (jnp.arange(top)[None, :] + offset_by) % top, axis=1)


def load_shares(number_of, total, bound, slope, full):
    weights = [(1 << 20) // math.isqrt(rank ** slope) + 1 for rank in range(1, number_of + 1)]
    largest = bound if full else min(bound, max(-(-total // number_of), total * weights[0] // sum(weights)))
    least = 1 if total - largest >= number_of - 1 else 0
    holding, rest = [largest] + [least] * (number_of - 1), total - largest - least * (number_of - 1)
    while rest > 0:
        free = [i for i in range(1, number_of) if holding[i] < largest] or [i for i in range(1, number_of) if holding[i] < bound]
        whole, remaining = sum([weights[i] for i in free]), rest
        for i in free:
            more = min(bound - holding[i], max(1, remaining * weights[i] // whole), rest)
            holding[i] = holding[i] + more
            rest = rest - more
    return np.array(holding)


def normal_values(rng, extent, width, most, pieces=(), held_as=jnp.bfloat16):
    factor_of = shard_levels(rng, extent, pieces, -0.22, 0.18) if pieces else 1.0
    values = jax.random.normal(rng, extent, jnp.float32) * width * factor_of
    return jnp.minimum(jnp.maximum(values, -most), most).astype(held_as)


def setup_inputs(seed: int = 0) -> dict:
    key_list = jax.random.split(jax.random.key(seed), 7)
    ens_state = draw_ens_state(jax.random.fold_in(key_list[6], 71), 0)
    ens_obs = draw_ens_obs(jax.random.fold_in(key_list[6], 71), 0)
    innov = normal_values(key_list[2], (MEMBERS, NOBS), 1.0, 6.0, ((0, 8), (1, 4)))
    state_coord = place_ends(jax.random.randint(key_list[3], (2, STATE), 0, 2 * LOC), jax.random.fold_in(key_list[3], 1), 0, (2 * LOC) - 1).astype(jnp.int32)
    obs_coord = place_ends(jax.random.randint(key_list[4], (2, NOBS), 0, 2 * LOC), jax.random.fold_in(key_list[4], 1), 0, (2 * LOC) - 1).astype(jnp.int32)
    obs_routes_keys = jax.random.split(jax.random.fold_in(key_list[5], 1), NOBK // OBK_REG)
    obs_routes_turns = jax.random.permutation(jax.random.fold_in(key_list[5], 3), NOBK // OBK_REG)
    obs_routes = jax.vmap(lambda own, number: assign_block(jax.random.fold_in(key_list[5], 2), own, number, OBK_REG, N_REG, 1, CAP, 2))(obs_routes_keys, obs_routes_turns).reshape((NOBK, 1))
    return dict(ens_state=ens_state, ens_obs=ens_obs, innov=innov, state_coord=state_coord, obs_coord=obs_coord, obs_routes=obs_routes)


def slot_table(routes, regions, per_region, capacity):
    target = routes[:, 0].reshape(regions, per_region)
    hits = (target[:, :, None] == jnp.arange(regions, dtype=jnp.int32)[None, None, :]).astype(jnp.int32)
    order = jnp.cumsum(hits, axis=1) - 1
    chosen = hits[:, :, :, None] * (order[:, :, :, None] == jnp.arange(capacity, dtype=jnp.int32)[None, None, None, :]).astype(jnp.int32)
    listed = lax.optimization_barrier(jnp.sum(chosen * jnp.arange(per_region, dtype=jnp.int32)[None, :, None, None], axis=1))
    filled = lax.optimization_barrier(jnp.sum(chosen, axis=1))
    return (listed, filled)

def taper_weight(dist_sq):
    ratio = jnp.sqrt(dist_sq) / LOC
    clipped = jnp.maximum(ratio, 1.0)
    inner = (((-0.25 * ratio + 0.5) * ratio + 0.625) * ratio - 5.0 / 3.0) * ratio * ratio + 1.0
    outer = ((((ratio / 12.0 - 0.5) * ratio + 0.625) * ratio + 5.0 / 3.0) * ratio - 5.0) * ratio + 4.0 - 2.0 / (3.0 * clipped)
    return jnp.where(ratio <= 1.0, inner, jnp.where(ratio < 2.0, outer, 0.0))

def reference(ens_state, ens_obs, innov, state_coord, obs_coord, obs_routes):
    members = ens_state.shape[0]
    state_wide = ens_state.astype(jnp.float32)
    state_anom = (state_wide - lax.optimization_barrier(jnp.mean(state_wide, axis=0, keepdims=True))).astype(jnp.bfloat16)
    obs_wide = ens_obs.astype(jnp.float32)
    obs_anom = (obs_wide - lax.optimization_barrier(jnp.mean(obs_wide, axis=0, keepdims=True))).astype(jnp.bfloat16)
    listed, filled = slot_table(obs_routes, REGIONS, OBK_REG, CAP)
    obs_blocks = obs_anom.reshape(members, NOBK, BLK)
    innov_blocks = innov.reshape(members, NOBK, BLK)
    coord_blocks = obs_coord.reshape(2, NOBK, BLK)
    source = jnp.arange(REGIONS * CAP, dtype=jnp.int32) // CAP
    column = jnp.arange(REGIONS * CAP, dtype=jnp.int32) % CAP
    band_rows = SB_DEV * BLK

    def region(index):
        local = listed[source, index, column]
        present = filled[source, index, column].astype(jnp.bfloat16)
        block_ids = (source * OBK_REG + local).astype(jnp.int32)
        picked = jnp.take(obs_blocks, block_ids, axis=1) * present[None, :, None]
        weights = jnp.take(innov_blocks, block_ids, axis=1) * present[None, :, None]
        obs_xy = jnp.take(coord_blocks, block_ids, axis=1).reshape(2, BANDS, SLOTS * BLK)
        start = (index * STATE_REG).astype(jnp.int32)
        rows = lax.dynamic_slice_in_dim(state_anom, start, STATE_REG, 1)
        rows_xy = lax.dynamic_slice_in_dim(state_coord, start, STATE_REG, 1).reshape(2, BANDS, band_rows)
        rows_band = rows.reshape(members, BANDS, band_rows).astype(jnp.float32)
        picked_band = picked.reshape(members, BANDS, SLOTS * BLK).astype(jnp.float32)
        cov = jnp.einsum('jbi,jbq->biq', rows_band, picked_band) / (members - 1)
        delta_x = rows_xy[0][:, :, None] - obs_xy[0][:, None, :]
        delta_y = rows_xy[1][:, :, None] - obs_xy[1][:, None, :]
        dist_sq = (delta_x * delta_x + delta_y * delta_y).astype(jnp.float32)
        tiles = (cov * taper_weight(dist_sq)).astype(jnp.bfloat16)
        weights_band = weights.reshape(members, BANDS, SLOTS * BLK).astype(jnp.float32)
        increments = jnp.einsum('jbq,biq->jbi', weights_band, tiles.astype(jnp.float32))
        return increments.astype(jnp.bfloat16).reshape(members, STATE_REG)
    per_region = lax.map(region, jnp.arange(REGIONS, dtype=jnp.int32))
    increments = jnp.transpose(per_region, (1, 0, 2)).reshape(members, STATE)
    return (state_wide + increments.astype(jnp.float32)).astype(jnp.bfloat16)
```

```python
import functools

import jax
import jax.numpy as jnp
from jax import lax
from jax.experimental import pallas as pl
from jax.experimental.pallas import tpu as pltpu
from jax.sharding import PartitionSpec as P

BLK = 128
LOC = 32
SLOTS = 4


VMEM = pl.BlockSpec(memory_space=pltpu.VMEM)
SMEM = pl.BlockSpec(memory_space=pltpu.SMEM)
PARAMS = pltpu.CompilerParams(vmem_limit_bytes=16 << 20)


def list_blocks(routes_ref, listed_ref, source, per_region, regions, capacity):
    def clear(i, carry):
        listed_ref[i] = -1
        return carry

    lax.fori_loop(0, regions * capacity, clear, 0)

    def step(k, counts):
        r = routes_ref[source * per_region + k]
        c = jnp.int32(0)
        for i in range(regions):
            c = jnp.where(r == i, counts[i], c)
        listed_ref[r * capacity + c] = k
        return tuple(jnp.where(r == i, n + 1, n) for i, n in enumerate(counts))

    lax.fori_loop(0, per_region, step, (jnp.int32(0),) * regions)


def gather_kernel(dims, routes_ref, obs_ref, innov_ref, *refs):
    regions, per_region, capacity = dims
    outs, listed_ref = refs[:regions], refs[regions]
    me = lax.axis_index("reg")
    list_blocks(routes_ref, listed_ref, me, per_region, regions, capacity)
    for step, out_ref in enumerate(outs):
        target = lax.bitwise_xor(me, step)
        for c in range(capacity):
            k = listed_ref[target * capacity + c]
            columns = pl.ds(pl.multiple_of(jnp.maximum(k, 0) * BLK, BLK), BLK)
            for part, ref in enumerate((obs_ref, innov_ref)):
                block = ref[:, columns]
                at = (part * capacity + c) * BLK
                out_ref[:, at : at + BLK] = jnp.where(k >= 0, block, jnp.zeros_like(block))


def arrange_kernel(dims, *refs):
    regions, share, width = dims
    out_ref = refs[regions]
    me = lax.axis_index("reg")
    for step in range(regions):
        source = lax.bitwise_xor(me, step)
        for j in range(share):
            for part in range(2):
                at = (part * share + j) * width
                out_ref[source * share + j, :, part * width : (part + 1) * width] = refs[step][
                    :, at : at + width
                ]


def split_kernel(bands, state_ref, out_ref):
    width = out_ref.shape[2]
    for b in range(bands):
        out_ref[b] = state_ref[:, b * width : (b + 1) * width]


def taper_kernel(dims, routes_ref, rows_ref, obs_ref, out_ref, listed_ref):
    regions, per_region, capacity, share, scale = dims
    width = out_ref.shape[1]
    region, band = lax.axis_index("reg"), lax.axis_index("mem")
    source = band // share
    first = (band % share) * SLOTS
    list_blocks(routes_ref, listed_ref, source, per_region, regions, capacity)
    at = pl.multiple_of(band * width, BLK)
    row_x = rows_ref[0:1, pl.ds(at, width)].astype(jnp.float32)
    row_y = rows_ref[1:2, pl.ds(at, width)].astype(jnp.float32)
    for s in range(SLOTS):
        k = jnp.maximum(listed_ref[region * capacity + first + s], 0)
        block = pl.multiple_of((source * per_region + k) * BLK, BLK)
        xy = obs_ref[:, pl.ds(block, BLK)].astype(jnp.float32)
        col_x = jnp.transpose(jnp.broadcast_to(xy[0:1], (8, BLK)))[:, 0:1]
        col_y = jnp.transpose(jnp.broadcast_to(xy[1:2], (8, BLK)))[:, 0:1]
        dx = col_x - row_x
        dy = col_y - row_y
        dist_sq = dx * dx + dy * dy
        inverse = lax.rsqrt(jnp.maximum(dist_sq, 1.0))
        ratio = dist_sq * inverse * (1.0 / LOC)
        inner = (((-0.25 * ratio + 0.5) * ratio + 0.625) * ratio - 5.0 / 3.0) * ratio * ratio + 1.0
        outer = (
            ((((ratio / 12.0 - 0.5) * ratio + 0.625) * ratio + 5.0 / 3.0) * ratio - 5.0) * ratio
            + 4.0
            - (2.0 * LOC / 3.0) * inverse
        )
        weight = jnp.where(ratio <= 1.0, inner, jnp.where(ratio < 2.0, outer, 0.0))
        out_ref[s * BLK : (s + 1) * BLK, :] = weight * scale


def centered(values):
    wide = values.astype(jnp.float32)
    return (wide - jnp.mean(wide, axis=0, keepdims=True)).astype(jnp.bfloat16)


def update_kernel(state_ref, both_ref, taper_ref, out_ref):
    bands, mem_dev, width = state_ref.shape
    members = bands * mem_dev
    state_anom = centered(state_ref[...].reshape(members, width))
    obs_anom = centered(both_ref[:, :, :width].reshape(members, width))
    innov = both_ref[:, :, width:].reshape(members, width)
    cov = lax.dot_general(
        obs_anom, state_anom, (((0,), (0,)), ((), ())), preferred_element_type=jnp.float32
    )
    tiles = (cov * taper_ref[...]).astype(jnp.bfloat16)
    out = lax.dot_general(
        innov, tiles, (((1,), (0,)), ((), ())), preferred_element_type=jnp.float32
    )
    out_ref[...] = out.astype(jnp.bfloat16).reshape(bands, mem_dev, width)


def add_kernel(state_ref, inc_ref, out_ref):
    bands, _, width = inc_ref.shape
    for b in range(bands):
        cols = slice(b * width, (b + 1) * width)
        total = state_ref[:, cols].astype(jnp.float32) + inc_ref[b].astype(jnp.float32)
        out_ref[:, cols] = total.astype(jnp.bfloat16)


def call(kernel, shapes, in_specs, *args, scratch=(), name=None):
    outs = [jax.ShapeDtypeStruct(s, d) for s, d in shapes]
    single = len(outs) == 1
    return pl.pallas_call(
        kernel,
        out_shape=outs[0] if single else outs,
        in_specs=in_specs,
        out_specs=VMEM if single else [VMEM] * len(outs),
        scratch_shapes=list(scratch),
        compiler_params=PARAMS,
        name=name,
    )(*args)


def per_device(ens_state, ens_obs, innov, state_coord, obs_coord, obs_routes):
    regions = lax.axis_size("reg")
    bands = lax.axis_size("mem")
    mem_dev, columns = ens_state.shape
    members = mem_dev * bands
    per_region = ens_obs.shape[1] // BLK
    capacity = SLOTS * bands // regions
    share = bands // regions
    width = SLOTS * BLK
    band_rows = columns // bands
    bf16 = jnp.bfloat16
    routes = obs_routes.reshape(-1)
    listed = pltpu.SMEM((regions * capacity,), jnp.int32)

    picked = call(
        functools.partial(gather_kernel, (regions, per_region, capacity)),
        [((mem_dev, 2 * capacity * BLK), bf16)] * regions,
        [SMEM, VMEM, VMEM],
        routes,
        ens_obs,
        innov,
        scratch=[listed],
        name="gather",
    )
    received = [picked[0]]
    for step in range(1, regions):
        pairs = [(i, i ^ step) for i in range(regions)]
        received.append(lax.ppermute(picked[step], "reg", pairs))
    state_split = call(
        functools.partial(split_kernel, bands),
        [((bands, mem_dev, band_rows), bf16)],
        [VMEM],
        ens_state,
        name="split",
    )
    state_rows = lax.all_to_all(state_split, "mem", split_axis=0, concat_axis=0, tiled=True)
    taper = call(
        functools.partial(
            taper_kernel, (regions, per_region, capacity, share, 1.0 / (members - 1))
        ),
        [((width, band_rows), jnp.float32)],
        [SMEM, VMEM, VMEM],
        routes,
        state_coord,
        obs_coord,
        scratch=[listed],
        name="taper",
    )
    both = call(
        functools.partial(arrange_kernel, (regions, share, width)),
        [((bands, mem_dev, 2 * width), bf16)],
        [VMEM] * regions,
        *received,
        name="arrange",
    )
    both = lax.all_to_all(both, "mem", split_axis=0, concat_axis=0, tiled=True)
    increments = call(
        update_kernel,
        [((bands, mem_dev, band_rows), bf16)],
        [VMEM] * 3,
        state_rows,
        both,
        taper,
        name="update",
    )
    returned = lax.all_to_all(increments, "mem", split_axis=0, concat_axis=0, tiled=True)
    return call(
        add_kernel,
        [((mem_dev, columns), bf16)],
        [VMEM] * 2,
        ens_state,
        returned,
        name="add",
    )


def solution(mesh):
    return jax.shard_map(
        per_device,
        mesh=mesh,
        in_specs=(P("mem", "reg"), P("mem", "reg"), P("mem", "reg"), P(None, "reg"), P(), P()),
        out_specs=P("mem", "reg"),
        check_vma=False,
    )
```

```python
import functools
import math

import jax
import jax.numpy as jnp
from jax import lax
from jax.experimental import pallas as pl
from jax.experimental.pallas import tpu as pltpu
from jax.sharding import PartitionSpec as P


BLK = 128
LOC = 32
SLOTS = 4


VMEM = pl.BlockSpec(memory_space=pltpu.VMEM)
SMEM = pl.BlockSpec(memory_space=pltpu.SMEM)
HBM = pl.BlockSpec(memory_space=pltpu.HBM)
PARAMS = pltpu.CompilerParams(vmem_limit_bytes=16 << 20)


def list_blocks(routes_ref, listed_ref, base, per_region, regions, capacity):
    unroll = math.gcd(per_region, 16)

    def clear(i, carry):
        listed_ref[i] = -1
        return carry

    lax.fori_loop(0, regions * capacity, clear, 0, unroll=unroll)

    def step(k, counts):
        r = routes_ref[base + k]
        c = counts[0]
        for i in range(1, regions):
            c = jnp.where(r == i, counts[i], c)
        listed_ref[r * capacity + c] = k
        return tuple(jnp.where(r == i, n + 1, n) for i, n in enumerate(counts))

    lax.fori_loop(0, per_region, step, (jnp.int32(0),) * regions, unroll=unroll)


def gather_kernel(dims, routes_hbm, obs_hbm, innov_hbm, *refs):
    regions, per_region, capacity = dims
    outs = refs[:regions]
    routes_ref, obs_ref, innov_ref, listed_ref, sems = refs[regions:]
    me = lax.axis_index("reg")
    loads = [
        pltpu.make_async_copy(src, dst, sems.at[i])
        for i, (src, dst) in enumerate(
            ((routes_hbm, routes_ref), (obs_hbm, obs_ref), (innov_hbm, innov_ref))
        )
    ]
    for load in loads:
        load.start()
    loads[0].wait()
    list_blocks(routes_ref, listed_ref, me * per_region, per_region, regions, capacity)
    loads[1].wait()
    loads[2].wait()
    for step, out_ref in enumerate(outs):
        target = lax.bitwise_xor(me, step)
        for c in range(capacity):
            k = listed_ref[target * capacity + c]
            columns = pl.ds(pl.multiple_of(jnp.maximum(k, 0) * BLK, BLK), BLK)
            for part, ref in enumerate((obs_ref, innov_ref)):
                block = ref[:, columns]
                at = (part * capacity + c) * BLK
                out_ref[:, at : at + BLK] = jnp.where(k >= 0, block, jnp.zeros_like(block))


def arrange_kernel(dims, *refs):
    regions, share, width = dims
    out_ref = refs[regions]
    me = lax.axis_index("reg")
    for step in range(regions):
        source = lax.bitwise_xor(me, step)
        for j in range(share):
            for part in range(2):
                at = (part * share + j) * width
                out_ref[source * share + j, :, part * width : (part + 1) * width] = refs[step][
                    :, at : at + width
                ]


def split_kernel(bands, state_ref, out_ref):
    width = out_ref.shape[2]
    for b in range(bands):
        out_ref[b] = state_ref[:, b * width : (b + 1) * width]


def taper_kernel(dims, routes_ref, rows_ref, obs_ref, out_ref, listed_ref):
    regions, per_region, capacity, share, scale = dims
    width = out_ref.shape[1]
    region, band = lax.axis_index("reg"), lax.axis_index("mem")
    source = band // share
    first = (band % share) * SLOTS
    base = source * per_region
    list_blocks(routes_ref, listed_ref, base, per_region, regions, capacity)
    rows_at = pl.ds(pl.multiple_of(band * width, BLK), width)
    rows = terms(rows_ref[:, rows_at], -2.0 / (LOC * LOC), 1.0 / (LOC * LOC), False)
    for s in range(SLOTS):
        k = jnp.maximum(listed_ref[region * capacity + first + s], 0)
        block = pl.ds(pl.multiple_of((base + k) * BLK, BLK), BLK)
        columns = terms(obs_ref[:, block], 1.0, 1.0, True)
        square = lax.dot_general(
            columns, rows, (((0,), (0,)), ((), ())), preferred_element_type=jnp.float32
        )
        inverse = lax.rsqrt(jnp.maximum(square, 1.0 / (LOC * LOC)))
        ratio = square * inverse
        inner = (((-0.25 * scale) * ratio + 0.5 * scale) * ratio + 0.625 * scale) * ratio
        inner = (inner - 5.0 / 3.0 * scale) * square + scale
        rest = jnp.maximum(2.0 - ratio, 0.0)
        rest = rest * rest
        outer = ((scale / 12.0) * ratio + scale / 6.0) * ratio - scale / 24.0
        outer = outer * (rest * rest) * inverse
        out_ref[s * BLK : (s + 1) * BLK, :] = jnp.where(ratio <= 1.0, inner, outer)


def terms(xy, cross, unit, left):
    norm = xy[0:1] * xy[0:1] + xy[1:2] * xy[1:2]
    high = lax.bitwise_and(norm, -256)
    low = lax.bitwise_and(norm, 255)
    ones = jnp.ones_like(norm)
    own, other = [high, low], [ones, ones]
    order = own + other if left else other + own
    body = jnp.concatenate([xy] + order + [jnp.zeros_like(xy)], axis=0).astype(jnp.float32)
    at = lax.broadcasted_iota(jnp.int32, body.shape, 0)
    return (body * jnp.where(at < 2, cross, unit)).astype(jnp.bfloat16)


def centered(values):
    wide = values.astype(jnp.float32)
    return (wide - jnp.mean(wide, axis=0, keepdims=True)).astype(jnp.bfloat16)


def update_kernel(state_ref, both_ref, taper_ref, out_ref):
    bands, mem_dev, width = state_ref.shape
    members = bands * mem_dev
    state_anom = centered(state_ref[...].reshape(members, width))
    obs_anom = centered(both_ref[:, :, :width].reshape(members, width))
    innov = both_ref[:, :, width:].reshape(members, width)
    cov = lax.dot_general(
        obs_anom, state_anom, (((0,), (0,)), ((), ())), preferred_element_type=jnp.float32
    )
    tiles = (cov * taper_ref[...]).astype(jnp.bfloat16)
    out = lax.dot_general(
        innov, tiles, (((1,), (0,)), ((), ())), preferred_element_type=jnp.float32
    )
    out_ref[...] = out.astype(jnp.bfloat16).reshape(bands, mem_dev, width)


def add_kernel(state_ref, inc_ref, out_ref):
    bands, _, width = inc_ref.shape
    for b in range(bands):
        cols = slice(b * width, (b + 1) * width)
        total = state_ref[:, cols].astype(jnp.float32) + inc_ref[b].astype(jnp.float32)
        out_ref[:, cols] = total.astype(jnp.bfloat16)


def call(kernel, shapes, in_specs, *args, scratch=()):
    outs = [jax.ShapeDtypeStruct(s, d) for s, d in shapes]
    single = len(outs) == 1
    return pl.pallas_call(
        kernel,
        out_shape=outs[0] if single else outs,
        in_specs=in_specs,
        out_specs=VMEM if single else [VMEM] * len(outs),
        scratch_shapes=list(scratch),
        compiler_params=PARAMS,
    )(*args)


def per_device(ens_state, ens_obs, innov, state_coord, obs_coord, obs_routes):
    regions = lax.axis_size("reg")
    bands = lax.axis_size("mem")
    mem_dev, columns = ens_state.shape
    members = mem_dev * bands
    per_region = ens_obs.shape[1] // BLK
    capacity = SLOTS * bands // regions
    share = bands // regions
    width = SLOTS * BLK
    band_rows = columns // bands
    bf16 = jnp.bfloat16
    routes = obs_routes.reshape(-1)
    listed = pltpu.SMEM((regions * capacity,), jnp.int32)

    picked = call(
        functools.partial(gather_kernel, (regions, per_region, capacity)),
        [((mem_dev, 2 * capacity * BLK), bf16)] * regions,
        [HBM] * 3,
        *(pltpu.with_memory_space_constraint(x, pltpu.HBM) for x in (routes, ens_obs, innov)),
        scratch=[
            pltpu.SMEM(routes.shape, jnp.int32),
            pltpu.VMEM(ens_obs.shape, bf16),
            pltpu.VMEM(innov.shape, bf16),
            listed,
            pltpu.SemaphoreType.DMA((3,)),
        ],
    )
    received = [picked[0]]
    for step in range(1, regions):
        pairs = [(i, i ^ step) for i in range(regions)]
        received.append(lax.ppermute(picked[step], "reg", pairs))
    state_split = call(
        functools.partial(split_kernel, bands),
        [((bands, mem_dev, band_rows), bf16)],
        [VMEM],
        ens_state,
    )
    state_rows = lax.all_to_all(state_split, "mem", split_axis=0, concat_axis=0, tiled=True)
    taper = call(
        functools.partial(
            taper_kernel, (regions, per_region, capacity, share, 1.0 / (members - 1))
        ),
        [((width, band_rows), jnp.float32)],
        [SMEM, VMEM, VMEM],
        routes,
        state_coord,
        obs_coord,
        scratch=[listed],
    )
    both = call(
        functools.partial(arrange_kernel, (regions, share, width)),
        [((bands, mem_dev, 2 * width), bf16)],
        [VMEM] * regions,
        *received,
    )
    both = lax.all_to_all(both, "mem", split_axis=0, concat_axis=0, tiled=True)
    increments = call(
        update_kernel, [((bands, mem_dev, band_rows), bf16)], [VMEM] * 3, state_rows, both, taper
    )
    returned = lax.all_to_all(increments, "mem", split_axis=0, concat_axis=0, tiled=True)
    return call(add_kernel, [((mem_dev, columns), bf16)], [VMEM] * 2, ens_state, returned)


def solution(mesh):
    return jax.shard_map(
        per_device,
        mesh=mesh,
        in_specs=(P("mem", "reg"), P("mem", "reg"), P("mem", "reg"), P(None, "reg"), P(), P()),
        out_specs=P("mem", "reg"),
        check_vma=False,
    )
```

```python
import functools
import math

import jax
import jax.numpy as jnp
from jax import lax
from jax.experimental import pallas as pl
from jax.experimental.pallas import tpu as pltpu
from jax.sharding import PartitionSpec as P


BLK = 128
LOC = 32
SLOTS = 4


VMEM = pl.BlockSpec(memory_space=pltpu.VMEM)
SMEM = pl.BlockSpec(memory_space=pltpu.SMEM)
HBM = pl.BlockSpec(memory_space=pltpu.HBM)
PARAMS = pltpu.CompilerParams(vmem_limit_bytes=16 << 20)


def list_blocks(routes_ref, listed_ref, base, per_region, regions, capacity):
    unroll = math.gcd(per_region, 16)

    def clear(i, carry):
        listed_ref[i] = -1
        return carry

    lax.fori_loop(0, regions * capacity, clear, 0, unroll=unroll)

    def step(k, counts):
        r = routes_ref[base + k]
        c = counts[0]
        for i in range(1, regions):
            c = jnp.where(r == i, counts[i], c)
        listed_ref[r * capacity + c] = k
        return tuple(jnp.where(r == i, n + 1, n) for i, n in enumerate(counts))

    lax.fori_loop(0, per_region, step, (jnp.int32(0),) * regions, unroll=unroll)


def gather_kernel(dims, routes_hbm, obs_hbm, innov_hbm, *refs):
    regions, per_region, capacity = dims
    outs = refs[:regions]
    routes_ref, obs_ref, innov_ref, listed_ref, sems = refs[regions:]
    me = lax.axis_index("reg")
    loads = [
        pltpu.make_async_copy(src, dst, sems.at[i])
        for i, (src, dst) in enumerate(
            ((routes_hbm, routes_ref), (obs_hbm, obs_ref), (innov_hbm, innov_ref))
        )
    ]
    for load in loads:
        load.start()
    loads[0].wait()
    list_blocks(routes_ref, listed_ref, me * per_region, per_region, regions, capacity)
    loads[1].wait()
    loads[2].wait()
    for step, out_ref in enumerate(outs):
        target = lax.bitwise_xor(me, step)
        for c in range(capacity):
            k = listed_ref[target * capacity + c]
            columns = pl.ds(pl.multiple_of(jnp.maximum(k, 0) * BLK, BLK), BLK)
            for part, ref in enumerate((obs_ref, innov_ref)):
                block = ref[:, columns]
                at = (part * capacity + c) * BLK
                out_ref[:, at : at + BLK] = jnp.where(k >= 0, block, jnp.zeros_like(block))


def arrange_kernel(dims, state_ref, *refs):
    regions, share, rows, width = dims
    out_ref = refs[regions]
    me = lax.axis_index("reg")
    for b in range(regions * share):
        out_ref[b, :, :rows] = state_ref[:, b * rows : (b + 1) * rows]
    for step in range(regions):
        source = lax.bitwise_xor(me, step)
        for j in range(share):
            for part in range(2):
                at = (part * share + j) * width
                to = rows + part * width
                out_ref[source * share + j, :, to : to + width] = refs[step][:, at : at + width]


def taper_kernel(dims, routes_ref, rows_ref, obs_ref, out_ref, listed_ref):
    regions, per_region, capacity, share, scale = dims
    width = out_ref.shape[1]
    region, band = lax.axis_index("reg"), lax.axis_index("mem")
    source = band // share
    first = (band % share) * SLOTS
    base = source * per_region
    list_blocks(routes_ref, listed_ref, base, per_region, regions, capacity)
    rows_at = pl.ds(pl.multiple_of(band * width, BLK), width)
    rows = terms(rows_ref[:, rows_at], -2.0 / (LOC * LOC), 1.0 / (LOC * LOC), False)
    for s in range(SLOTS):
        k = jnp.maximum(listed_ref[region * capacity + first + s], 0)
        block = pl.ds(pl.multiple_of((base + k) * BLK, BLK), BLK)
        columns = terms(obs_ref[:, block], 1.0, 1.0, True)
        square = lax.dot_general(
            columns, rows, (((0,), (0,)), ((), ())), preferred_element_type=jnp.float32
        )
        inverse = lax.rsqrt(jnp.maximum(square, 1.0 / (LOC * LOC)))
        ratio = square * inverse
        inner = (((-0.25 * scale) * ratio + 0.5 * scale) * ratio + 0.625 * scale) * ratio
        inner = (inner - 5.0 / 3.0 * scale) * square + scale
        rest = jnp.maximum(2.0 - ratio, 0.0)
        rest = rest * rest
        outer = ((scale / 12.0) * ratio + scale / 6.0) * ratio - scale / 24.0
        outer = outer * (rest * rest) * inverse
        out_ref[s * BLK : (s + 1) * BLK, :] = jnp.where(ratio <= 1.0, inner, outer)


def terms(xy, cross, unit, left):
    norm = xy[0:1] * xy[0:1] + xy[1:2] * xy[1:2]
    high = lax.bitwise_and(norm, -256)
    low = lax.bitwise_and(norm, 255)
    ones = jnp.ones_like(norm)
    own, other = [high, low], [ones, ones]
    order = own + other if left else other + own
    body = jnp.concatenate([xy] + order + [jnp.zeros_like(xy)], axis=0).astype(jnp.float32)
    at = lax.broadcasted_iota(jnp.int32, body.shape, 0)
    return (body * jnp.where(at < 2, cross, unit)).astype(jnp.bfloat16)


def centered(values):
    wide = values.astype(jnp.float32)
    return (wide - jnp.mean(wide, axis=0, keepdims=True)).astype(jnp.bfloat16)


def update_kernel(all_ref, taper_ref, out_ref):
    bands, mem_dev, rows = out_ref.shape
    members = bands * mem_dev
    width = taper_ref.shape[0]
    state_anom = centered(all_ref[:, :, :rows].reshape(members, rows))
    obs_anom = centered(all_ref[:, :, rows : rows + width].reshape(members, width))
    innov = all_ref[:, :, rows + width :].reshape(members, width)
    cov = lax.dot_general(
        obs_anom, state_anom, (((0,), (0,)), ((), ())), preferred_element_type=jnp.float32
    )
    tiles = (cov * taper_ref[...]).astype(jnp.bfloat16)
    out = lax.dot_general(
        innov, tiles, (((1,), (0,)), ((), ())), preferred_element_type=jnp.float32
    )
    out_ref[...] = out.astype(jnp.bfloat16).reshape(bands, mem_dev, rows)


def add_kernel(state_ref, inc_ref, out_ref):
    bands, _, width = inc_ref.shape
    for b in range(bands):
        cols = slice(b * width, (b + 1) * width)
        total = state_ref[:, cols].astype(jnp.float32) + inc_ref[b].astype(jnp.float32)
        out_ref[:, cols] = total.astype(jnp.bfloat16)


def call(kernel, shapes, in_specs, *args, scratch=()):
    outs = [jax.ShapeDtypeStruct(s, d) for s, d in shapes]
    single = len(outs) == 1
    return pl.pallas_call(
        kernel,
        out_shape=outs[0] if single else outs,
        in_specs=in_specs,
        out_specs=VMEM if single else [VMEM] * len(outs),
        scratch_shapes=list(scratch),
        compiler_params=PARAMS,
    )(*args)


def per_device(ens_state, ens_obs, innov, state_coord, obs_coord, obs_routes):
    regions = lax.axis_size("reg")
    bands = lax.axis_size("mem")
    mem_dev, columns = ens_state.shape
    members = mem_dev * bands
    per_region = ens_obs.shape[1] // BLK
    capacity = SLOTS * bands // regions
    share = bands // regions
    width = SLOTS * BLK
    band_rows = columns // bands
    bf16 = jnp.bfloat16
    routes = obs_routes.reshape(-1)
    listed = pltpu.SMEM((regions * capacity,), jnp.int32)

    picked = call(
        functools.partial(gather_kernel, (regions, per_region, capacity)),
        [((mem_dev, 2 * capacity * BLK), bf16)] * regions,
        [HBM] * 3,
        *(pltpu.with_memory_space_constraint(x, pltpu.HBM) for x in (routes, ens_obs, innov)),
        scratch=[
            pltpu.SMEM(routes.shape, jnp.int32),
            pltpu.VMEM(ens_obs.shape, bf16),
            pltpu.VMEM(innov.shape, bf16),
            listed,
            pltpu.SemaphoreType.DMA((3,)),
        ],
    )
    received = [picked[0]]
    for step in range(1, regions):
        pairs = [(i, i ^ step) for i in range(regions)]
        received.append(lax.ppermute(picked[step], "reg", pairs))
    taper = call(
        functools.partial(
            taper_kernel, (regions, per_region, capacity, share, 1.0 / (members - 1))
        ),
        [((width, band_rows), jnp.float32)],
        [SMEM, VMEM, VMEM],
        routes,
        state_coord,
        obs_coord,
        scratch=[listed],
    )
    sent = call(
        functools.partial(arrange_kernel, (regions, share, band_rows, width)),
        [((bands, mem_dev, band_rows + 2 * width), bf16)],
        [VMEM] * (regions + 1),
        ens_state,
        *received,
    )
    ensemble = lax.all_to_all(sent, "mem", split_axis=0, concat_axis=0, tiled=True)
    increments = call(
        update_kernel, [((bands, mem_dev, band_rows), bf16)], [VMEM] * 2, ensemble, taper
    )
    returned = lax.all_to_all(increments, "mem", split_axis=0, concat_axis=0, tiled=True)
    return call(add_kernel, [((mem_dev, columns), bf16)], [VMEM] * 2, ens_state, returned)


def solution(mesh):
    return jax.shard_map(
        per_device,
        mesh=mesh,
        in_specs=(P("mem", "reg"), P("mem", "reg"), P("mem", "reg"), P(None, "reg"), P(), P()),
        out_specs=P("mem", "reg"),
        check_vma=False,
    )
```

```python
import functools
import math

import jax
import jax.numpy as jnp
from jax import lax
from jax.experimental import pallas as pl
from jax.experimental.pallas import tpu as pltpu
from jax.sharding import PartitionSpec as P


BLK = 128
LOC = 32
SLOTS = 4
CORES = 2


VMEM = pl.BlockSpec(memory_space=pltpu.VMEM)
SMEM = pl.BlockSpec(memory_space=pltpu.SMEM)
PARAMS = pltpu.CompilerParams(vmem_limit_bytes=16 << 20)


def list_blocks(routes_ref, listed_ref, base, per_region, regions, capacity):
    unroll = math.gcd(per_region, 16)

    def clear(i, carry):
        listed_ref[i] = -1
        return carry

    lax.fori_loop(0, regions * capacity, clear, 0, unroll=unroll)

    def step(k, counts):
        r = routes_ref[base + k]
        c = counts[0]
        for i in range(1, regions):
            c = jnp.where(r == i, counts[i], c)
        listed_ref[r * capacity + c] = k
        return tuple(jnp.where(r == i, n + 1, n) for i, n in enumerate(counts))

    lax.fori_loop(0, per_region, step, (jnp.int32(0),) * regions, unroll=unroll)


def load_kernel(*refs):
    half = len(refs) // 2
    sems = refs[-1]
    loads = [
        pltpu.make_async_copy(refs[i], refs[half + i], sems.at[i]) for i in range(half)
    ]
    for load in loads:
        load.start()
    for load in loads:
        load.wait()


def gather_kernel(dims, routes_ref, *refs):
    regions, per_region, capacity, share, chips = dims
    obs, innov, state = refs[0:2], refs[2:4], refs[4:6]
    routed, rows_out = refs[6 : 6 + regions], refs[6 + regions : 6 + regions + chips]
    listed_ref = refs[-1]
    members, rows = obs[0].shape[0], rows_out[0].shape[1]
    me, band = lax.axis_index("reg"), lax.axis_index("mem")
    chip, core = band // CORES, band % CORES
    list_blocks(routes_ref, listed_ref, me * per_region, per_region, regions, capacity)
    for step, out_ref in enumerate(routed):
        target = lax.bitwise_xor(me, step)
        for j in range(share // CORES):
            first = target * capacity + (j * CORES + core) * SLOTS
            for c in range(SLOTS):
                k = listed_ref[first + c]
                columns = pl.ds(pl.multiple_of(jnp.maximum(k, 0) * BLK, BLK), BLK)
                for part, pair in enumerate((obs, innov)):
                    at = ((j * 2 + part) * SLOTS + c) * BLK
                    for half, ref in enumerate(pair):
                        block = ref[:, columns]
                        block = jnp.where(k >= 0, block, jnp.zeros_like(block))
                        out_ref[half * members : (half + 1) * members, at : at + BLK] = block
    for step, out_ref in enumerate(rows_out):
        to = lax.bitwise_xor(chip, step) * CORES + core
        columns = pl.ds(pl.multiple_of(to * rows, BLK), rows)
        for half, ref in enumerate(state):
            out_ref[half * members : (half + 1) * members, :] = ref[:, columns]


def arrange_kernel(dims, *refs):
    regions, share = dims
    routed, outs = refs[:regions], refs[regions:]
    width = outs[0].shape[1]
    me, band = lax.axis_index("reg"), lax.axis_index("mem")
    chip, core = band // CORES, band % CORES
    for step, out_ref in enumerate(outs):
        to = lax.bitwise_xor(chip, step) * CORES + core
        held = lax.bitwise_xor(to // share, me)
        at = pl.multiple_of((to % share) // CORES * width, BLK)
        for t in range(regions):

            @pl.when(held == t)
            def _(ref=routed[t], out_ref=out_ref, at=at):
                out_ref[...] = ref[:, pl.ds(at, width)]


def taper_kernel(dims, routes_ref, rows_ref, obs_ref, out_ref, listed_ref):
    regions, per_region, capacity, share, scale = dims
    width = out_ref.shape[1]
    region, band = lax.axis_index("reg"), lax.axis_index("mem")
    source = band // share
    first = (band % share) * SLOTS
    base = source * per_region
    list_blocks(routes_ref, listed_ref, base, per_region, regions, capacity)
    rows_at = pl.ds(pl.multiple_of(band * width, BLK), width)
    rows = terms(rows_ref[:, rows_at], -2.0 / (LOC * LOC), 1.0 / (LOC * LOC), False)
    for s in range(SLOTS):
        k = jnp.maximum(listed_ref[region * capacity + first + s], 0)
        block = pl.ds(pl.multiple_of((base + k) * BLK, BLK), BLK)
        columns = terms(obs_ref[:, block], 1.0, 1.0, True)
        square = lax.dot_general(
            columns, rows, (((0,), (0,)), ((), ())), preferred_element_type=jnp.float32
        )
        inverse = lax.rsqrt(jnp.maximum(square, 1.0 / (LOC * LOC)))
        ratio = square * inverse
        inner = (((-0.25 * scale) * ratio + 0.5 * scale) * ratio + 0.625 * scale) * ratio
        inner = (inner - 5.0 / 3.0 * scale) * square + scale
        rest = jnp.maximum(2.0 - ratio, 0.0)
        rest = rest * rest
        outer = ((scale / 12.0) * ratio + scale / 6.0) * ratio - scale / 24.0
        outer = outer * (rest * rest) * inverse
        out_ref[s * BLK : (s + 1) * BLK, :] = jnp.where(ratio <= 1.0, inner, outer)


def terms(xy, cross, unit, left):
    norm = xy[0:1] * xy[0:1] + xy[1:2] * xy[1:2]
    high = lax.bitwise_and(norm, -256)
    low = lax.bitwise_and(norm, 255)
    ones = jnp.ones_like(norm)
    own, other = [high, low], [ones, ones]
    order = own + other if left else other + own
    body = jnp.concatenate([xy] + order + [jnp.zeros_like(xy)], axis=0).astype(jnp.float32)
    at = lax.broadcasted_iota(jnp.int32, body.shape, 0)
    return (body * jnp.where(at < 2, cross, unit)).astype(jnp.bfloat16)


def centered(values):
    wide = values.astype(jnp.float32)
    return (wide - jnp.mean(wide, axis=0, keepdims=True)).astype(jnp.bfloat16)


def update_kernel(chips, *refs):
    state, both = refs[:chips], refs[chips : 2 * chips]
    taper_ref, outs = refs[2 * chips], refs[2 * chips + 1 :]
    members, width = state[0].shape[0], taper_ref.shape[0]
    state_anom = centered(jnp.concatenate([ref[...] for ref in state], axis=0))
    obs_anom = centered(jnp.concatenate([ref[:, :width] for ref in both], axis=0))
    innov = jnp.concatenate([ref[:, width:] for ref in both], axis=0)
    cov = lax.dot_general(
        obs_anom, state_anom, (((0,), (0,)), ((), ())), preferred_element_type=jnp.float32
    )
    tiles = (cov * taper_ref[...]).astype(jnp.bfloat16)
    out = lax.dot_general(
        innov, tiles, (((1,), (0,)), ((), ())), preferred_element_type=jnp.float32
    ).astype(jnp.bfloat16)
    for k, out_ref in enumerate(outs):
        out_ref[...] = out[k * members : (k + 1) * members]


def swap_kernel(*refs):
    out_ref = refs[-1]
    members = out_ref.shape[1]
    for k, ref in enumerate(refs[:-1]):
        out_ref[k] = ref[members:, :]


def add_kernel(chips, state_ref, *refs):
    own, other_ref, out_ref = refs[:chips], refs[chips], refs[chips + 1]
    _, members, rows = other_ref.shape
    band = lax.axis_index("mem")
    chip, core = band // CORES, band % CORES
    for k in range(chips):
        first = lax.bitwise_xor(chip, k) * CORES
        for which, inc in ((core, own[k][:members, :]), (CORES - 1 - core, other_ref[k])):
            columns = pl.ds(pl.multiple_of((first + which) * rows, BLK), rows)
            total = state_ref[:, columns].astype(jnp.float32) + inc.astype(jnp.float32)
            out_ref[:, columns] = total.astype(jnp.bfloat16)


def call(kernel, shapes, in_specs, *args, scratch=()):
    outs = [jax.ShapeDtypeStruct(s, d) for s, d in shapes]
    single = len(outs) == 1
    result = pl.pallas_call(
        kernel,
        out_shape=outs[0] if single else outs,
        in_specs=in_specs,
        out_specs=VMEM if single else [VMEM] * len(outs),
        scratch_shapes=list(scratch),
        compiler_params=PARAMS,
    )(*args)
    return result if single else list(result)


def swap(value, axis, step):
    pairs = [(i, i ^ step) for i in range(lax.axis_size(axis))]
    return lax.ppermute(value, axis, pairs)


def per_device(ens_state, ens_obs, innov, state_coord, obs_coord, obs_routes):
    regions = lax.axis_size("reg")
    bands = lax.axis_size("mem")
    mem_dev, columns = ens_state.shape
    members = mem_dev * bands
    per_region = ens_obs.shape[1] // BLK
    capacity = SLOTS * bands // regions
    share = bands // regions
    chips = bands // CORES
    width = SLOTS * BLK
    rows = columns // bands
    held = CORES * mem_dev
    bf16 = jnp.bfloat16
    listed = pltpu.SMEM((regions * capacity,), jnp.int32)

    obs_other = swap(ens_obs, "mem", 1)
    innov_other = swap(innov, "mem", 1)
    state_other = swap(ens_state, "mem", 1)
    own = (ens_obs, innov, ens_state, obs_routes.reshape(-1))
    ens_obs, innov, ens_state, routes = call(
        load_kernel,
        [(x.shape, x.dtype) for x in own],
        [pl.BlockSpec(memory_space=pltpu.HBM)] * len(own),
        *(pltpu.with_memory_space_constraint(x, pltpu.HBM) for x in own),
        scratch=[pltpu.SemaphoreType.DMA((len(own),))],
    )
    picked = call(
        functools.partial(gather_kernel, (regions, per_region, capacity, share, chips)),
        [((held, share // CORES * 2 * width), bf16)] * regions + [((held, rows), bf16)] * chips,
        [SMEM] + [VMEM] * 6,
        routes,
        ens_obs,
        obs_other,
        innov,
        innov_other,
        ens_state,
        state_other,
        scratch=[listed],
    )
    routed, state = picked[:regions], picked[regions:]
    for step in range(1, regions):
        routed[step] = swap(routed[step], "reg", step)
    for k in range(1, chips):
        state[k] = swap(state[k], "mem", k * CORES)
    taper = call(
        functools.partial(
            taper_kernel, (regions, per_region, capacity, share, 1.0 / (members - 1))
        ),
        [((width, rows), jnp.float32)],
        [SMEM, VMEM, VMEM],
        routes,
        state_coord,
        obs_coord,
        scratch=[listed],
    )
    both = call(
        functools.partial(arrange_kernel, (regions, share)),
        [((held, 2 * width), bf16)] * chips,
        [VMEM] * regions,
        *routed,
    )
    for k in range(1, chips):
        both[k] = swap(both[k], "mem", k * CORES)
    increments = call(
        functools.partial(update_kernel, chips),
        [((held, rows), bf16)] * chips,
        [VMEM] * (2 * chips + 1),
        *state,
        *both,
        taper,
    )
    for k in range(1, chips):
        increments[k] = swap(increments[k], "mem", k * CORES)
    other = call(swap_kernel, [((chips, mem_dev, rows), bf16)], [VMEM] * chips, *increments)
    other = swap(other, "mem", 1)
    return call(
        functools.partial(add_kernel, chips),
        [((mem_dev, columns), bf16)],
        [VMEM] * (chips + 2),
        ens_state,
        *increments,
        other,
    )


def solution(mesh):
    return jax.shard_map(
        per_device,
        mesh=mesh,
        in_specs=(P("mem", "reg"), P("mem", "reg"), P("mem", "reg"), P(None, "reg"), P(), P()),
        out_specs=P("mem", "reg"),
        check_vma=False,
    )
```

```python
import functools
import math

import jax
import jax.numpy as jnp
from jax import lax
from jax.experimental import pallas as pl
from jax.experimental.pallas import tpu as pltpu
from jax.sharding import PartitionSpec as P


BLK = 128
LOC = 32
SLOTS = 4
CORES = 2


VMEM = pl.BlockSpec(memory_space=pltpu.VMEM)
SMEM = pl.BlockSpec(memory_space=pltpu.SMEM)
PARAMS = pltpu.CompilerParams(vmem_limit_bytes=16 << 20)


def list_blocks(routes_ref, listed_ref, base, per_region, regions, capacity):
    unroll = math.gcd(per_region, 16)

    def clear(i, carry):
        listed_ref[i] = -1
        return carry

    lax.fori_loop(0, regions * capacity, clear, 0, unroll=unroll)

    def step(k, counts):
        r = routes_ref[base + k]
        c = counts[0]
        for i in range(1, regions):
            c = jnp.where(r == i, counts[i], c)
        listed_ref[r * capacity + c] = k
        return tuple(jnp.where(r == i, n + 1, n) for i, n in enumerate(counts))

    lax.fori_loop(0, per_region, step, (jnp.int32(0),) * regions, unroll=unroll)


def load_kernel(*refs):
    half = len(refs) // 2
    sems = refs[-1]
    loads = [
        pltpu.make_async_copy(refs[i], refs[half + i], sems.at[i]) for i in range(half)
    ]
    for load in loads:
        load.start()
    for load in loads:
        load.wait()


def gather_kernel(dims, routes_ref, *refs):
    regions, per_region, capacity, share, chips = dims
    obs, innov, state = refs[0:2], refs[2:4], refs[4:6]
    routed, rows_out = refs[6 : 6 + regions], refs[6 + regions : 6 + regions + chips]
    listed_ref = refs[-1]
    members, rows = obs[0].shape[0], rows_out[0].shape[1]
    me, band = lax.axis_index("reg"), lax.axis_index("mem")
    chip, core = band // CORES, band % CORES
    list_blocks(routes_ref, listed_ref, me * per_region, per_region, regions, capacity)
    for step, out_ref in enumerate(routed):
        hop = int(step != 0)
        target = lax.bitwise_xor(me, step)
        for j in range(share // CORES):
            to = me * (share // CORES) + j
            parity = jnp.where(to == chip, lax.bitwise_xor(core, hop), lax.bitwise_xor(core, 1 - hop))
            first = target * capacity + (j * CORES + parity) * SLOTS
            for c in range(SLOTS):
                k = listed_ref[first + c]
                columns = pl.ds(pl.multiple_of(jnp.maximum(k, 0) * BLK, BLK), BLK)
                for part, pair in enumerate((obs, innov)):
                    at = ((j * 2 + part) * SLOTS + c) * BLK
                    for half, ref in enumerate(pair):
                        block = ref[:, columns]
                        block = jnp.where(k >= 0, block, jnp.zeros_like(block))
                        row = (half ^ hop) * members
                        out_ref[row : row + members, at : at + BLK] = block
    for step, out_ref in enumerate(rows_out):
        parity = lax.bitwise_xor(core, int(step != 0))
        to = lax.bitwise_xor(chip, step) * CORES + parity
        columns = pl.ds(pl.multiple_of(to * rows, BLK), rows)
        for half, ref in enumerate(state):
            out_ref[half * members : (half + 1) * members, :] = ref[:, columns]


def arrange_kernel(dims, *refs):
    regions, share = dims
    routed, outs = refs[:regions], refs[regions:]
    width = outs[0].shape[1]
    me, chip = lax.axis_index("reg"), lax.axis_index("mem") // CORES
    for step, out_ref in enumerate(outs):
        to = lax.bitwise_xor(chip, step)
        held = lax.bitwise_xor(to // (share // CORES), me)
        at = pl.multiple_of(to % (share // CORES) * width, BLK)
        for t in range(regions):

            @pl.when(held == t)
            def _(ref=routed[t], out_ref=out_ref, at=at):
                out_ref[...] = ref[:, pl.ds(at, width)]


def taper_kernel(dims, routes_ref, rows_ref, obs_ref, out_ref, listed_ref):
    regions, per_region, capacity, share, scale = dims
    width = out_ref.shape[1]
    region, band = lax.axis_index("reg"), lax.axis_index("mem")
    source = band // share
    first = (band % share) * SLOTS
    base = source * per_region
    list_blocks(routes_ref, listed_ref, base, per_region, regions, capacity)
    rows_at = pl.ds(pl.multiple_of(band * width, BLK), width)
    rows = terms(rows_ref[:, rows_at], -2.0 / (LOC * LOC), 1.0 / (LOC * LOC), False)
    for s in range(SLOTS):
        k = jnp.maximum(listed_ref[region * capacity + first + s], 0)
        block = pl.ds(pl.multiple_of((base + k) * BLK, BLK), BLK)
        columns = terms(obs_ref[:, block], 1.0, 1.0, True)
        square = lax.dot_general(
            columns, rows, (((0,), (0,)), ((), ())), preferred_element_type=jnp.float32
        )
        inverse = lax.rsqrt(jnp.maximum(square, 1.0 / (LOC * LOC)))
        ratio = square * inverse
        inner = (((-0.25 * scale) * ratio + 0.5 * scale) * ratio + 0.625 * scale) * ratio
        inner = (inner - 5.0 / 3.0 * scale) * square + scale
        rest = jnp.maximum(2.0 - ratio, 0.0)
        rest = rest * rest
        outer = ((scale / 12.0) * ratio + scale / 6.0) * ratio - scale / 24.0
        outer = outer * (rest * rest) * inverse
        out_ref[s * BLK : (s + 1) * BLK, :] = jnp.where(ratio <= 1.0, inner, outer)


def terms(xy, cross, unit, left):
    norm = xy[0:1] * xy[0:1] + xy[1:2] * xy[1:2]
    high = lax.bitwise_and(norm, -256)
    low = lax.bitwise_and(norm, 255)
    ones = jnp.ones_like(norm)
    own, other = [high, low], [ones, ones]
    order = own + other if left else other + own
    body = jnp.concatenate([xy] + order + [jnp.zeros_like(xy)], axis=0).astype(jnp.float32)
    at = lax.broadcasted_iota(jnp.int32, body.shape, 0)
    return (body * jnp.where(at < 2, cross, unit)).astype(jnp.bfloat16)


def centered(values):
    wide = values.astype(jnp.float32)
    return (wide - jnp.mean(wide, axis=0, keepdims=True)).astype(jnp.bfloat16)


def update_kernel(chips, *refs):
    state, both = refs[:chips], refs[chips : 2 * chips]
    taper_ref, outs = refs[2 * chips], refs[2 * chips + 1 :]
    members, width = state[0].shape[0], taper_ref.shape[0]
    state_anom = centered(jnp.concatenate([ref[...] for ref in state], axis=0))
    obs_anom = centered(jnp.concatenate([ref[:, :width] for ref in both], axis=0))
    innov = jnp.concatenate([ref[:, width:] for ref in both], axis=0)
    cov = lax.dot_general(
        obs_anom, state_anom, (((0,), (0,)), ((), ())), preferred_element_type=jnp.float32
    )
    tiles = (cov * taper_ref[...]).astype(jnp.bfloat16)
    out = lax.dot_general(
        innov, tiles, (((1,), (0,)), ((), ())), preferred_element_type=jnp.float32
    ).astype(jnp.bfloat16)
    for k, out_ref in enumerate(outs):
        out_ref[...] = out[k * members : (k + 1) * members]


def swap_kernel(*refs):
    out_ref = refs[-1]
    members = out_ref.shape[1]
    for k, ref in enumerate(refs[:-1]):
        out_ref[k] = ref[members:, :]


def add_kernel(chips, state_ref, *refs):
    own, other_ref, out_ref = refs[:chips], refs[chips], refs[chips + 1]
    _, members, rows = other_ref.shape
    band = lax.axis_index("mem")
    chip, core = band // CORES, band % CORES
    for k in range(chips):
        first = lax.bitwise_xor(chip, k) * CORES
        parity = lax.bitwise_xor(core, int(k != 0))
        for which, inc in ((parity, own[k][:members, :]), (1 - parity, other_ref[k])):
            columns = pl.ds(pl.multiple_of((first + which) * rows, BLK), rows)
            total = state_ref[:, columns].astype(jnp.float32) + inc.astype(jnp.float32)
            out_ref[:, columns] = total.astype(jnp.bfloat16)


def call(kernel, shapes, in_specs, *args, scratch=()):
    outs = [jax.ShapeDtypeStruct(s, d) for s, d in shapes]
    single = len(outs) == 1
    result = pl.pallas_call(
        kernel,
        out_shape=outs[0] if single else outs,
        in_specs=in_specs,
        out_specs=VMEM if single else [VMEM] * len(outs),
        scratch_shapes=list(scratch),
        compiler_params=PARAMS,
    )(*args)
    return result if single else list(result)


def swap(value, mem=0, reg=0):
    bands, regions = lax.axis_size("mem"), lax.axis_size("reg")
    devices = [(m, r) for m in range(bands) for r in range(regions)]
    pairs = [(m * regions + r, (m ^ mem) * regions + (r ^ reg)) for m, r in devices]
    return lax.ppermute(value, ("mem", "reg"), pairs)


def per_device(ens_state, ens_obs, innov, state_coord, obs_coord, obs_routes):
    regions = lax.axis_size("reg")
    bands = lax.axis_size("mem")
    mem_dev, columns = ens_state.shape
    members = mem_dev * bands
    per_region = ens_obs.shape[1] // BLK
    capacity = SLOTS * bands // regions
    share = bands // regions
    chips = bands // CORES
    width = SLOTS * BLK
    rows = columns // bands
    held = CORES * mem_dev
    bf16 = jnp.bfloat16
    listed = pltpu.SMEM((regions * capacity,), jnp.int32)

    obs_other = swap(ens_obs, mem=1)
    innov_other = swap(innov, mem=1)
    state_other = swap(ens_state, mem=1)
    own = (ens_obs, innov, ens_state, obs_routes.reshape(-1))
    ens_obs, innov, ens_state, routes = call(
        load_kernel,
        [(x.shape, x.dtype) for x in own],
        [pl.BlockSpec(memory_space=pltpu.HBM)] * len(own),
        *(pltpu.with_memory_space_constraint(x, pltpu.HBM) for x in own),
        scratch=[pltpu.SemaphoreType.DMA((len(own),))],
    )
    picked = call(
        functools.partial(gather_kernel, (regions, per_region, capacity, share, chips)),
        [((held, share // CORES * 2 * width), bf16)] * regions + [((held, rows), bf16)] * chips,
        [SMEM] + [VMEM] * 6,
        routes,
        ens_obs,
        obs_other,
        innov,
        innov_other,
        ens_state,
        state_other,
        scratch=[listed],
    )
    routed, state = picked[:regions], picked[regions:]
    for step in range(1, regions):
        routed[step] = swap(routed[step], mem=1, reg=step)
    for k in range(1, chips):
        state[k] = swap(state[k], mem=k * CORES + 1)
    taper = call(
        functools.partial(
            taper_kernel, (regions, per_region, capacity, share, 1.0 / (members - 1))
        ),
        [((width, rows), jnp.float32)],
        [SMEM, VMEM, VMEM],
        routes,
        state_coord,
        obs_coord,
        scratch=[listed],
    )
    both = call(
        functools.partial(arrange_kernel, (regions, share)),
        [((held, 2 * width), bf16)] * chips,
        [VMEM] * regions,
        *routed,
    )
    for k in range(1, chips):
        both[k] = swap(both[k], mem=k * CORES + 1)
    increments = call(
        functools.partial(update_kernel, chips),
        [((held, rows), bf16)] * chips,
        [VMEM] * (2 * chips + 1),
        *state,
        *both,
        taper,
    )
    for k in range(1, chips):
        increments[k] = swap(increments[k], mem=k * CORES + 1)
    other = call(swap_kernel, [((chips, mem_dev, rows), bf16)], [VMEM] * chips, *increments)
    other = swap(other, mem=1)
    return call(
        functools.partial(add_kernel, chips),
        [((mem_dev, columns), bf16)],
        [VMEM] * (chips + 2),
        ens_state,
        *increments,
        other,
    )


def solution(mesh):
    return jax.shard_map(
        per_device,
        mesh=mesh,
        in_specs=(P("mem", "reg"), P("mem", "reg"), P("mem", "reg"), P(None, "reg"), P(), P()),
        out_specs=P("mem", "reg"),
        check_vma=False,
    )
```
